32 devices in a mesh: fsdp: 32 (over z, y, x, core).
Axes of the slice: x: 2, y: 2, z: 4, core: 2. Of those that a mesh axis runs over, the one named last changes fastest.
Arguments:
- hidden_in: bfloat16 [2, 32768, 768], P(None, 'fsdp'), may hold values from -26 to 26
- doc_lens: int32 [2, 32, 2], P(None, 'fsdp'), may hold values from 1 to 768, 1024 in all within a row
- w_qkv: bfloat16 [1769472], P('fsdp'), may hold values from -0.21875 to 0.21875
- w_out: bfloat16 [589824], P('fsdp'), may hold values from -0.21875 to 0.21875
- w_fc1: bfloat16 [2359296], P('fsdp'), may hold values from -0.21875 to 0.21875
- w_fc2: bfloat16 [2359296], P('fsdp'), may hold values from -0.109375 to 0.109375
- vec_params: bfloat16 [16896], P('fsdp'), may hold values from -1.5 to 1.5
- cotangent: bfloat16 [2, 32768, 768], P(None, 'fsdp'), may hold values from -6 to 6
Outputs:
- hidden_out: bfloat16 [2, 32768, 768], P(None, 'fsdp')
- input_grad: bfloat16 [2, 32768, 768], P(None, 'fsdp')
- grad_qkv: float32 [1769472], P('fsdp')
- grad_out: float32 [589824], P('fsdp')
- grad_fc1: float32 [2359296], P('fsdp')
- grad_fc2: float32 [2359296], P('fsdp')
- grad_vec: float32 [16896], P('fsdp')
The draws below stay inside these ranges and needn't reach their ends.
Inputs may be any that keep to these rules, and one draw needn't show every extreme that they name: `doc_lens`: the 2 lengths of one sequence sum to 1024.
All inputs are finite; a program needn't handle non-finite values.
Results may differ from the reference program's by a relative error of at most 0.008.
Values may be sent and summed in bfloat16 or wider, within the bound.
No kernel may reach another device: no remote copies, remote signals or barrier semaphores. Data moves between devices by JAX's collectives and lax.ppermute only.
A program may use at most 448 MiB of HBM per device.

```python
import math
import jax
import jax.numpy as jnp
import numpy as np
from jax import lax

D = 768
HEADS = 12
HEAD_DIM = 64
FF = 3072
BLOCK = 256
DOCS = 2
SEQ = 1024
MICRO = 2
DOC_MOST = 768
ROWS = 32768
GROUPS = 32
N_FSDP = 32


def draw_hidden_in(key, part):
    first, second, third = jax.random.split(key, 3)
    array_shape = (MICRO, ROWS, D)
    baseline = jnp.clip(jax.random.normal(first, array_shape, jnp.float32), -4.0, 4.0)
    row_scale = jnp.exp(jax.random.uniform(second, (MICRO, ROWS, 1), jnp.float32, -1.15, 1.15))
    col_scale = jnp.exp(jax.random.uniform(third, (D,), jnp.float32, -0.7, 0.7))
    return (baseline * row_scale * col_scale).astype(jnp.bfloat16)


def draw_vec_params(key, part):
    first, second = jax.random.split(key)
    total = 10 * D + 3 * FF
    places = jnp.arange(total, dtype=jnp.int32)
    is_gain = (places < D) | (places >= 4 * D) & (places < 5 * D) | (places >= 7 * D) & (places < 8 * D) | (places >= 9 * D + FF) & (places < 9 * D + 2 * FF)
    spread = jax.random.uniform(first, (total,), jnp.float32, -1.0, 1.0)
    offsets = jnp.clip(jax.random.normal(second, (total,), jnp.float32) * 0.5, -1.5, 1.5)
    return jnp.where(is_gain, 1.0 + 0.4 * spread, offsets).astype(jnp.bfloat16)


def level_of(key, extent, cuts, least, largest):
    level = 1.0
    for position, parts in cuts:
        steps = jax.random.uniform(jax.random.fold_in(jax.random.fold_in(key, 6), position), (parts,), jnp.float32, least / len(cuts), largest / len(cuts))
        level = level * jnp.repeat(jnp.exp(steps), extent[position] // parts).reshape((-1,) + (1,) * (len(extent) - 1 - position))
    return level


def length_profile(number_of, total, most, slope):
    weights = [(1 << 20) // math.isqrt(standing ** slope) + 1 for standing in range(2, number_of + 1)]
    spare, holding = total - most - (number_of - 1), [1] * (number_of - 1)
    while spare > 0:
        movable = [i for i in range(number_of - 1) if holding[i] < most]
        whole, left = sum([weights[i] for i in movable]), spare
        for i in movable:
            extra = min(most - holding[i], max(1, left * weights[i] // whole), spare)
            holding[i] = holding[i] + extra
            spare = spare - extra
    return np.array([most] + holding)


def uneven_parts(rng, amount, total, reach, lean):
    if amount == 2:
        one = jax.random.randint(rng, (), max(1, total - reach), min(reach, total - 1) + 1)
        return jnp.stack([one, total - one])
    sizes = jnp.asarray(length_profile(amount, total, reach, lean), jnp.int32)
    twos = (amount - 1) // 2
    source_of, taker = sizes[1:1 + 2 * twos:2], sizes[2:2 + 2 * twos:2]
    room = jnp.minimum(source_of - 1, reach - taker)
    passed = jax.random.randint(jax.random.fold_in(rng, 1), (twos,), 0, 1 << 20) % (room + 1)
    sizes = sizes.at[1:1 + 2 * twos:2].set(source_of - passed).at[2:2 + 2 * twos:2].set(taker + passed)
    return sizes[jax.random.permutation(jax.random.fold_in(rng, 2), amount)]


def noise(rng, extent, scale, reach, shards=(), kind=jnp.bfloat16):
    loudness = level_of(rng, extent, shards, -0.22, 0.18) if shards else 1.0
    array = jax.random.normal(rng, extent, jnp.float32) * scale * loudness
    return jnp.minimum(jnp.maximum(array, -reach), reach).astype(kind)


def setup_inputs(seed: int = 0) -> dict:
    seeds = jax.random.split(jax.random.key(seed), 9)
    return {
        "hidden_in": draw_hidden_in(jax.random.fold_in(seeds[8], 71), 0),
        "doc_lens": jax.vmap(lambda own: uneven_parts(own, DOCS, SEQ, DOC_MOST, 0))(jax.random.split(seeds[1], MICRO * GROUPS)).reshape((MICRO, GROUPS, DOCS)).astype(jnp.int32),
        "w_qkv": noise(seeds[2], (3 * D * D,), D ** -0.5, 0.21875, ((0, 32),)),
        "w_out": noise(seeds[3], (D * D,), D ** -0.5, 0.21875, ((0, 32),)),
        "w_fc1": noise(seeds[4], (D * FF,), D ** -0.5, 0.21875, ((0, 32),)),
        "w_fc2": noise(seeds[5], (FF * D,), FF ** -0.5, 0.109375, ((0, 32),)),
        "vec_params": draw_vec_params(jax.random.fold_in(seeds[8], 71), 0),
        "cotangent": noise(seeds[7], (MICRO, ROWS, D), 1.0, 6.0, ((1, 32),)),
    }


@jax.custom_vjp
def low(v):
    return lax.optimization_barrier(v.astype(jnp.bfloat16)).astype(jnp.float32)

@jax.custom_vjp
def low_back(v):
    return v

def low_keep(v):
    return (low(v), None)

def low_pass(kept, grad):
    return (grad,)

def back_keep(v):
    return (v, None)

def back_low(kept, grad):
    return (low(grad),)
low.defvjp(low_keep, low_pass)
low_back.defvjp(back_keep, back_low)
EPSILON = 1e-05
HIGHEST = lax.Precision.HIGHEST
MASKED_SCORE = -1e+30

def layer_norm(inputs, factor, offset):
    average = lax.optimization_barrier(jnp.mean(inputs, axis=-1, keepdims=True))
    centred = inputs - average
    variance = lax.optimization_barrier(jnp.mean(centred * centred, axis=-1, keepdims=True))
    return centred * lax.rsqrt(variance + EPSILON) * factor + offset

def visible_mask(lengths, seq_len):
    places = jnp.arange(seq_len, dtype=jnp.int32)
    doc_ends = jnp.cumsum(lengths).astype(jnp.int32)
    doc_starts = (doc_ends - lengths).astype(jnp.int32)
    doc_index = lax.optimization_barrier(jnp.sum((places[:, None] >= doc_ends[None, :]).astype(jnp.int32), axis=1)).astype(jnp.int32)
    member = doc_index[:, None] == jnp.arange(lengths.shape[0], dtype=jnp.int32)[None, :]
    doc_first = lax.optimization_barrier(jnp.sum(jnp.where(member, doc_starts[None, :], 0), axis=1)).astype(jnp.int32)
    block_index = (places - doc_first) // BLOCK
    same_doc = doc_index[:, None] == doc_index[None, :]
    return same_doc & (block_index[None, :] <= block_index[:, None])

def split_vector(vector, model_width, hidden):
    sizes_list = [model_width] * 9 + [hidden] * 3 + [model_width]
    pieces = []
    offset = 0
    for length in sizes_list:
        pieces.append(vector[offset:offset + length])
        offset += length
    return pieces

def sequence_layer(params, inputs, lengths):
    mat_qkv, mat_out, mat_fc1, mat_fc2, vector = params
    seq_len, model_width = inputs.shape
    hidden = mat_fc1.shape[1]
    ln1_gain, ln1_bias, q_bias, v_bias, attn_gain, attn_bias, out_bias, ln2_gain, ln2_bias, fc1_bias, ffn_gain, ffn_bias, fc2_bias = split_vector(vector, model_width, hidden)
    normed = low(layer_norm(inputs, ln1_gain, ln1_bias))
    projected = jnp.dot(normed, mat_qkv, precision=HIGHEST, preferred_element_type=jnp.float32)
    query = low(low_back(projected[:, :model_width] + q_bias))
    key_rows = low(low_back(projected[:, model_width:2 * model_width]))
    value_rows = low(low_back(projected[:, 2 * model_width:] + v_bias))
    query_heads = query.reshape(seq_len, HEADS, HEAD_DIM)
    key_heads = key_rows.reshape(seq_len, HEADS, HEAD_DIM)
    value_heads = value_rows.reshape(seq_len, HEADS, HEAD_DIM)
    scores = jnp.einsum('qhd,khd->hqk', query_heads, key_heads, precision=HIGHEST) * HEAD_DIM ** (-0.5)
    scores = low_back(scores)
    visible = visible_mask(lengths, seq_len)
    scores = jnp.where(visible[None], scores, MASKED_SCORE)
    row_top = lax.optimization_barrier(jnp.max(scores, axis=-1, keepdims=True))
    exponent = jnp.exp(scores - row_top)
    probabilities = low(exponent / lax.optimization_barrier(jnp.sum(exponent, axis=-1, keepdims=True)))
    attended = jnp.einsum('hqk,khd->qhd', probabilities, value_heads, precision=HIGHEST).reshape(seq_len, model_width)
    attended = low_back(attended)
    mixed_rows = low(layer_norm(attended, attn_gain, attn_bias))
    branch_attn = low_back(jnp.dot(mixed_rows, mat_out, precision=HIGHEST, preferred_element_type=jnp.float32) + out_bias)
    after_attn = inputs + branch_attn
    normed_two = low(layer_norm(after_attn, ln2_gain, ln2_bias))
    preact = low_back(jnp.dot(normed_two, mat_fc1, precision=HIGHEST, preferred_element_type=jnp.float32) + fc1_bias)
    inner_rows = low(layer_norm(jax.nn.gelu(preact, approximate=False), ffn_gain, ffn_bias))
    return after_attn + jnp.dot(inner_rows, mat_fc2, precision=HIGHEST, preferred_element_type=jnp.float32) + fc2_bias

def reference(hidden_in, doc_lens, w_qkv, w_out, w_fc1, w_fc2, vec_params, cotangent):
    model_width = hidden_in.shape[-1]
    seq_count = MICRO * N_FSDP
    group_size = math.gcd(seq_count, max(1, 4096 // SEQ))
    group_count = seq_count // group_size
    inputs = hidden_in.astype(jnp.float32).reshape(group_count, group_size, SEQ, model_width)
    cot_all = cotangent.astype(jnp.float32).reshape(group_count, group_size, SEQ, model_width)
    lengths = doc_lens.reshape(group_count, group_size, DOCS).astype(jnp.int32)
    params = (w_qkv.astype(jnp.float32).reshape(model_width, 3 * model_width), w_out.astype(jnp.float32).reshape(model_width, model_width), w_fc1.astype(jnp.float32).reshape(model_width, FF), w_fc2.astype(jnp.float32).reshape(FF, model_width), vec_params.astype(jnp.float32))

    def group_layer(chosen, block_in, block_len):
        return jax.vmap(lambda one_in, one_len: sequence_layer(chosen, one_in, one_len))(block_in, block_len)

    def scan_step(totals, pieces):
        block_in, block_cot, block_len = pieces
        outputs, pullback = jax.vjp(lambda chosen, moved: group_layer(chosen, moved, block_len), params, block_in)
        param_grads, input_grads = pullback(block_cot)
        totals = jax.tree.map(lambda first_arr, second_arr: first_arr + second_arr, totals, param_grads)
        return (totals, (outputs.astype(jnp.bfloat16), input_grads.astype(jnp.bfloat16)))
    initial = jax.tree.map(jnp.zeros_like, params)
    totals, (outputs, input_grads) = lax.scan(scan_step, initial, (inputs, cot_all, lengths))
    hidden_out = outputs.reshape(MICRO, N_FSDP * SEQ, model_width)
    input_grad = input_grads.reshape(MICRO, N_FSDP * SEQ, model_width)
    return (hidden_out, input_grad, totals[0].reshape(-1), totals[1].reshape(-1), totals[2].reshape(-1), totals[3].reshape(-1), totals[4])
```

```python
import functools

import jax
import jax.numpy as jnp
from jax import lax
from jax.experimental import pallas as pl
from jax.experimental.pallas import tpu as pltpu
from jax.sharding import PartitionSpec as P

HEADS = 12
HEAD_DIM = 64
BLOCK = 256

EPSILON = 1e-05
MASKED_SCORE = -1e30
BF = jnp.bfloat16
F32 = jnp.float32
TILE = 128
LIMIT = 64 * 1024 * 1024 - 1024 * 1024


def params(limit=LIMIT):
    return pltpu.CompilerParams(vmem_limit_bytes=limit)


def cost(flops, bytes_accessed, transcendentals=0):
    return pl.CostEstimate(
        flops=int(flops), bytes_accessed=int(bytes_accessed), transcendentals=int(transcendentals)
    )


def whole(shape):
    zeros = (0,) * len(shape)
    return pl.BlockSpec(shape, lambda *_: zeros, pipeline_mode=pl.Buffered(1))


def rows(height, width):
    return pl.BlockSpec((height, width), lambda i: (i, 0))


def standardize(v):
    average = jnp.mean(v, axis=-1, keepdims=True)
    centred = v - average
    variance = jnp.mean(centred * centred, axis=-1, keepdims=True)
    scale = lax.rsqrt(variance + EPSILON)
    return centred * scale, scale


def norm_backward(grad, gain, unit, scale):
    weighted = grad * gain
    first = jnp.mean(weighted, axis=-1, keepdims=True)
    second = jnp.mean(weighted * unit, axis=-1, keepdims=True)
    return scale * (weighted - first - unit * second)


def dot(a, b, contract):
    return lax.dot_general(a, b, ((contract[:1], contract[1:]), ((), ())), preferred_element_type=F32)


def fold(v):
    return jnp.sum(v.reshape(v.shape[0] // 8, 8, v.shape[1]), axis=0)


def project_body(x_ref, w_ref, vec_ref, out_ref):
    width = x_ref.shape[1]
    unit, _ = standardize(x_ref[...].astype(F32))
    normed = (unit * vec_ref[0:1, :] + vec_ref[1:2, :]).astype(BF)
    q = dot(normed, w_ref[:, :width], (1, 0)) + vec_ref[2:3, :]
    out_ref[:, :width] = (q * HEAD_DIM**-0.5).astype(BF)
    out_ref[:, width : 2 * width] = dot(normed, w_ref[:, width : 2 * width], (1, 0)).astype(BF)
    v = dot(normed, w_ref[:, 2 * width :], (1, 0)) + vec_ref[3:4, :]
    out_ref[:, 2 * width :] = v.astype(BF)


def project(x, w, vec):
    count, width = x.shape
    height = 512
    return pl.pallas_call(
        project_body,
        grid=(count // height,),
        in_specs=[rows(height, width), whole(w.shape), whole(vec.shape)],
        out_specs=rows(height, w.shape[1]),
        out_shape=jax.ShapeDtypeStruct((count, w.shape[1]), BF),
        compiler_params=params(),
        cost_estimate=cost(2 * count * w.size, 2 * (x.size + w.size + count * w.shape[1])),
        name="project",
    )(x, w, vec)


def key_span(lens_ref, seq, tile, tiles):
    length = lens_ref[seq, 0]
    total = tiles * TILE
    first = tile * TILE
    last = first + TILE - 1
    start = jnp.where(first < length, 0, length)
    end_one = jnp.minimum(((last >> 8) + 1) << 8, length)
    end_two = jnp.minimum(length + ((((last - length) >> 8) + 1) << 8), total)
    end = jnp.where(last < length, end_one, end_two)
    low = start >> 7
    high = (end + TILE - 1) >> 7
    count = jnp.maximum(high - low, 2)
    low = jnp.minimum(low, tiles - count)
    return low, count


def fill_bias(lens_ref, bias_ref, seq, tiles):
    length = lens_ref[seq, 0]
    total = tiles * TILE

    def one(tile, carry):
        low, count = key_span(lens_ref, seq, tile, tiles)
        query = tile * TILE + lax.broadcasted_iota(jnp.int32, (1, TILE), 1)
        early = query < length
        start = jnp.where(early, 0, length)
        end_one = jnp.minimum(((query >> 8) + 1) << 8, length)
        end_two = jnp.minimum(length + ((((query - length) >> 8) + 1) << 8), total)
        end = jnp.where(early, end_one, end_two)
        key = low * TILE + lax.broadcasted_iota(jnp.int32, (total, 1), 0)
        seen = (key >= start) & (key < end)
        bias_ref[tile] = jnp.where(seen, 0.0, MASKED_SCORE)
        return carry

    lax.fori_loop(0, tiles, one, 0)


def split_heads(v):
    lane = lax.broadcasted_iota(jnp.int32, v.shape, 1)
    zero = jnp.zeros_like(v)
    return jnp.concatenate(
        [jnp.where(lane < HEAD_DIM, v, zero), jnp.where(lane < HEAD_DIM, zero, v)], axis=0
    )


def join_heads(v):
    return jnp.concatenate([v[:HEAD_DIM, :TILE], v[HEAD_DIM:, TILE:]], axis=0)


def attend_body(lens_ref, q_ref, k_ref, v_ref, o_ref, lse_ref, bias_ref, vt_ref):
    seq, pair = pl.program_id(0), pl.program_id(1)
    tiles = q_ref.shape[0] // TILE

    @pl.when(pair == 0)
    def _():
        fill_bias(lens_ref, bias_ref, seq, tiles)

    vt_ref[...] = v_ref[...].T

    def one(tile, carry):
        low, count = key_span(lens_ref, seq, tile, tiles)
        at = pl.multiple_of(low * TILE, TILE)
        here = pl.multiple_of(tile * TILE, TILE)

        def variant(blocks):
            size = blocks * TILE
            q = split_heads(q_ref[pl.ds(here, TILE), :])
            scores = dot(k_ref[pl.ds(at, size), :], q, (1, 1))
            bias = bias_ref[tile, :size, :]
            scores = scores + jnp.concatenate([bias, bias], axis=1)
            top = jnp.max(scores, axis=0, keepdims=True)
            exponent = jnp.exp(scores - top)
            total = jnp.sum(exponent, axis=0, keepdims=True)
            mixed = dot(vt_ref[:, pl.ds(at, size)], exponent.astype(BF), (1, 0)) / total
            o_ref[pl.ds(here, TILE), :] = join_heads(mixed).T
            lse_ref[0, pl.ds(tile, 1), :] = top + jnp.log(total)

        for blocks in range(2, tiles + 1):
            pl.when(count == blocks)(functools.partial(variant, blocks))
        return carry

    lax.fori_loop(0, tiles, one, 0)


def attend(lens, qkv, length):
    count = qkv.shape[0]
    seqs = count // length
    pairs = HEADS // 2
    tiles = length // TILE
    take = lambda part: pl.BlockSpec((length, TILE), lambda s, p, *_: (s, part * pairs + p))
    grid_spec = pltpu.PrefetchScalarGridSpec(
        num_scalar_prefetch=1,
        grid=(seqs, pairs),
        in_specs=[take(0), take(1), take(2)],
        out_specs=[
            pl.BlockSpec((length, TILE), lambda s, p, *_: (s, p)),
            pl.BlockSpec((1, tiles, 2 * TILE), lambda s, p, *_: (s * pairs + p, 0, 0)),
        ],
        scratch_shapes=[pltpu.VMEM((tiles, length, TILE), F32), pltpu.VMEM((TILE, length), BF)],
    )
    return pl.pallas_call(
        attend_body,
        grid_spec=grid_spec,
        out_shape=[
            jax.ShapeDtypeStruct((count, HEADS * HEAD_DIM), F32),
            jax.ShapeDtypeStruct((seqs * pairs, tiles, 2 * TILE), F32),
        ],
        compiler_params=params(),
        cost_estimate=cost(12 * count * length * HEADS * HEAD_DIM, 12 * count * HEADS * HEAD_DIM),
        name="attend",
    )(lens, qkv, qkv, qkv)


def attend_back_body(
    lens_ref, q_ref, k_ref, v_ref, g_ref, lse_ref, inner_ref,
    dq_ref, dk_ref, dv_ref, sum_ref, bias_ref, kt_ref, dk_acc, dv_acc, row_ref,
):
    seq, pair = pl.program_id(0), pl.program_id(1)
    tiles = q_ref.shape[0] // TILE

    @pl.when(pair == 0)
    def _():
        fill_bias(lens_ref, bias_ref, seq, tiles)

    for head in range(2):
        line = inner_ref[pl.ds(2 * pair + head, 1), :]
        for tile in range(tiles):
            row_ref[tile : tile + 1, head * TILE : (head + 1) * TILE] = line[
                :, tile * TILE : (tile + 1) * TILE
            ]
    kt_ref[...] = k_ref[...].T
    dk_acc[...] = jnp.zeros_like(dk_acc)
    dv_acc[...] = jnp.zeros_like(dv_acc)

    def one(tile, carry):
        low, count = key_span(lens_ref, seq, tile, tiles)
        at = pl.multiple_of(low * TILE, TILE)
        here = pl.multiple_of(tile * TILE, TILE)

        def variant(blocks):
            size = blocks * TILE
            q = split_heads(q_ref[pl.ds(here, TILE), :])
            g = split_heads(g_ref[pl.ds(here, TILE), :])
            scores = dot(k_ref[pl.ds(at, size), :], q, (1, 1))
            bias = bias_ref[tile, :size, :]
            scores = scores + jnp.concatenate([bias, bias], axis=1)
            weights = jnp.exp(scores - lse_ref[0, pl.ds(tile, 1), :])
            grad = dot(v_ref[pl.ds(at, size), :], g, (1, 1))
            ds = (weights * (grad - row_ref[pl.ds(tile, 1), :])).astype(BF)
            dv_acc[pl.ds(at, size), :] += dot(weights.astype(BF), g, (1, 0))
            dk_acc[pl.ds(at, size), :] += dot(ds, q, (1, 0))
            dq = join_heads(dot(kt_ref[:, pl.ds(at, size)], ds, (1, 0))).T
            dq_ref[pl.ds(here, TILE), :] = (dq * HEAD_DIM**-0.5).astype(BF)

        for blocks in range(2, tiles + 1):
            pl.when(count == blocks)(functools.partial(variant, blocks))
        return carry

    lax.fori_loop(0, tiles, one, 0)
    dk_ref[...] = dk_acc[...].astype(BF)
    dv_ref[...] = dv_acc[...].astype(BF)
    sum_ref[0, 0:1, :] = jnp.sum(dq_ref[...].astype(F32), axis=0, keepdims=True)
    sum_ref[0, 1:2, :] = jnp.sum(dk_ref[...].astype(F32), axis=0, keepdims=True)
    sum_ref[0, 2:3, :] = jnp.sum(dv_ref[...].astype(F32), axis=0, keepdims=True)


def attend_back(lens, qkv, grads, lse, inner, length):
    count = qkv.shape[0]
    seqs = count // length
    pairs = HEADS // 2
    tiles = length // TILE
    width = HEADS * HEAD_DIM
    take = lambda part: pl.BlockSpec((length, TILE), lambda s, p, *_: (s, part * pairs + p))
    grid_spec = pltpu.PrefetchScalarGridSpec(
        num_scalar_prefetch=1,
        grid=(seqs, pairs),
        in_specs=[
            take(0), take(1), take(2), take(0),
            pl.BlockSpec((1, tiles, 2 * TILE), lambda s, p, *_: (s * pairs + p, 0, 0)),
            pl.BlockSpec((inner.shape[0], length), lambda s, p, *_: (0, s)),
        ],
        out_specs=[
            take(0), take(0), take(0),
            pl.BlockSpec((1, 8, TILE), lambda s, p, *_: (s, 0, p)),
        ],
        scratch_shapes=[
            pltpu.VMEM((tiles, length, TILE), F32),
            pltpu.VMEM((TILE, length), BF),
            pltpu.VMEM((length, TILE), F32),
            pltpu.VMEM((length, TILE), F32),
            pltpu.VMEM((tiles, 2 * TILE), F32),
        ],
    )
    return pl.pallas_call(
        attend_back_body,
        grid_spec=grid_spec,
        out_shape=[jax.ShapeDtypeStruct((count, width), BF)] * 3
        + [jax.ShapeDtypeStruct((seqs, 8, width), F32)],
        compiler_params=params(),
        cost_estimate=cost(30 * count * length * width, 14 * count * width),
        name="attend_back",
    )(lens, qkv, qkv, qkv, grads, lse, inner)


def middle_one_body(
    o_ref, x_ref, wo_ref, w1_ref, vec_ref, wide_ref,
    a_ref, x1_ref, h2_ref, a2_ref, unit_ref, slope_ref, act_ref, der_ref,
):
    unit, _ = standardize(o_ref[...])
    a = (unit * vec_ref[0:1, :] + vec_ref[1:2, :]).astype(BF)
    a_ref[...] = a
    x1 = x_ref[...].astype(F32) + dot(a, wo_ref[...], (1, 0)) + vec_ref[2:3, :]
    x1_ref[...] = x1
    unit, _ = standardize(x1)
    h2 = (unit * vec_ref[3:4, :] + vec_ref[4:5, :]).astype(BF)
    h2_ref[...] = h2
    height, hidden = act_ref.shape
    part = 512
    total = jnp.zeros((height, 128), F32)
    for start in range(0, hidden, part):
        cols = slice(start, start + part)
        f = dot(h2, w1_ref[:, cols], (1, 0)) + wide_ref[0:1, cols]
        cdf = 0.5 * (1.0 + lax.erf(f * 0.7071067811865476))
        pdf = 0.3989422804014327 * jnp.exp(-0.5 * f * f)
        act = f * cdf
        act_ref[:, cols] = act
        der_ref[:, cols] = cdf + f * pdf
        for at in range(0, part, 128):
            total = total + act[:, at : at + 128]
    average = jnp.sum(total, axis=-1, keepdims=True) / hidden
    total = jnp.zeros((height, 128), F32)
    for start in range(0, hidden, 128):
        centred = act_ref[:, start : start + 128] - average
        total = total + centred * centred
    scale = lax.rsqrt(jnp.sum(total, axis=-1, keepdims=True) / hidden + EPSILON)
    for start in range(0, hidden, part):
        cols = slice(start, start + part)
        unit = (act_ref[:, cols] - average) * scale
        unit_ref[:, cols] = unit.astype(BF)
        a2_ref[:, cols] = (unit * wide_ref[1:2, cols] + wide_ref[2:3, cols]).astype(BF)
        slope_ref[:, cols] = (der_ref[:, cols] * scale).astype(BF)


def middle_one(o, x, wo, w1, vec, wide):
    count, width = x.shape
    hidden = w1.shape[1]
    height = 256
    return pl.pallas_call(
        middle_one_body,
        grid=(count // height,),
        in_specs=[
            rows(height, width), rows(height, width), whole(wo.shape), whole(w1.shape),
            whole(vec.shape), whole(wide.shape),
        ],
        out_specs=[rows(height, width)] * 3 + [rows(height, hidden)] * 3,
        out_shape=[
            jax.ShapeDtypeStruct((count, width), BF),
            jax.ShapeDtypeStruct((count, width), F32),
            jax.ShapeDtypeStruct((count, width), BF),
        ]
        + [jax.ShapeDtypeStruct((count, hidden), BF)] * 3,
        scratch_shapes=[pltpu.VMEM((height, hidden), F32)] * 2,
        compiler_params=params(),
        cost_estimate=cost(2 * count * (wo.size + w1.size), 6 * count * hidden, 2 * count * hidden),
        name="middle_one",
    )(o, x, wo, w1, vec, wide)


def middle_two_body(
    a2_ref, unit_ref, slope_ref, x1_ref, e_ref, o_ref, w2_ref, w1_ref, wo_ref, vec_ref, wide_ref,
    out_ref, df_ref, dx1_ref, dr_ref, do_ref, inner_ref, sums_ref, wsums_ref, grad_ref,
):
    @pl.when(pl.program_id(0) == 0)
    def _():
        sums_ref[...] = jnp.zeros_like(sums_ref)
        wsums_ref[...] = jnp.zeros_like(wsums_ref)

    height, hidden = grad_ref.shape
    part = 512
    x1 = x1_ref[...]
    e = e_ref[...]
    e_wide = e.astype(F32)
    out_ref[...] = (x1 + dot(a2_ref[...], w2_ref[...], (1, 0)) + vec_ref[5:6, :]).astype(BF)
    sums_ref[0] += fold(e_wide)
    first = jnp.zeros((height, 128), F32)
    second = jnp.zeros((height, 128), F32)
    for start in range(0, hidden, part):
        cols = slice(start, start + part)
        grad = dot(e, w2_ref[cols, :], (1, 1))
        unit = unit_ref[:, cols].astype(F32)
        wsums_ref[0, :, cols] += fold(grad)
        wsums_ref[1, :, cols] += fold(grad * unit)
        grad = grad * wide_ref[1:2, cols]
        grad_ref[:, cols] = grad
        scaled = grad * unit
        for at in range(0, part, 128):
            first = first + grad[:, at : at + 128]
            second = second + scaled[:, at : at + 128]
    first = jnp.sum(first, axis=-1, keepdims=True) / hidden
    second = jnp.sum(second, axis=-1, keepdims=True) / hidden
    dh2 = jnp.zeros_like(x1)
    for start in range(0, hidden, part):
        cols = slice(start, start + part)
        unit = unit_ref[:, cols].astype(F32)
        df = ((grad_ref[:, cols] - first - unit * second) * slope_ref[:, cols].astype(F32)).astype(BF)
        df_ref[:, cols] = df
        wsums_ref[2, :, cols] += fold(df.astype(F32))
        dh2 = dh2 + dot(df, w1_ref[:, cols], (1, 1))
    unit, scale = standardize(x1)
    sums_ref[1] += fold(dh2 * unit)
    sums_ref[2] += fold(dh2)
    dx1 = e_wide + norm_backward(dh2, vec_ref[3:4, :], unit, scale)
    dx1_ref[...] = dx1
    dr = dx1.astype(BF)
    dr_ref[...] = dr
    sums_ref[3] += fold(dr.astype(F32))
    da = dot(dr, wo_ref[...], (1, 1))
    o = o_ref[...]
    unit, scale = standardize(o)
    sums_ref[4] += fold(da * unit)
    sums_ref[5] += fold(da)
    do = norm_backward(da, vec_ref[0:1, :], unit, scale).astype(BF)
    do_ref[...] = do
    product = do.astype(F32) * o
    high = product.astype(BF)
    low = (product - high.astype(F32)).astype(BF)
    head = lax.broadcasted_iota(jnp.int32, (16, product.shape[1]), 0)
    lane = lax.broadcasted_iota(jnp.int32, (16, product.shape[1]), 1)
    pick = jnp.where((lane >= head * HEAD_DIM) & (lane < (head + 1) * HEAD_DIM), 1.0, 0.0).astype(BF)
    inner_ref[...] = dot(pick, high, (1, 1)) + dot(pick, low, (1, 1))


def middle_two(a2, unit, slope, x1, e, o, w2, w1, wo, vec, wide):
    count, width = x1.shape
    hidden = w1.shape[1]
    height = 256
    return pl.pallas_call(
        middle_two_body,
        grid=(count // height,),
        in_specs=[rows(height, hidden)] * 3
        + [rows(height, width)] * 3
        + [whole(v.shape) for v in (w2, w1, wo, vec, wide)],
        out_specs=[
            rows(height, width), rows(height, hidden), rows(height, width), rows(height, width),
            rows(height, width),
            pl.BlockSpec((16, height), lambda i: (0, i)),
            pl.BlockSpec((6, 8, width), lambda i: (0, 0, 0)),
            pl.BlockSpec((3, 8, hidden), lambda i: (0, 0, 0)),
        ],
        out_shape=[
            jax.ShapeDtypeStruct((count, width), BF),
            jax.ShapeDtypeStruct((count, hidden), BF),
            jax.ShapeDtypeStruct((count, width), F32),
            jax.ShapeDtypeStruct((count, width), BF),
            jax.ShapeDtypeStruct((count, width), BF),
            jax.ShapeDtypeStruct((16, count), F32),
            jax.ShapeDtypeStruct((6, 8, width), F32),
            jax.ShapeDtypeStruct((3, 8, hidden), F32),
        ],
        scratch_shapes=[pltpu.VMEM((height, hidden), F32)],
        compiler_params=params(),
        cost_estimate=cost(2 * count * (wo.size + 3 * w1.size), 10 * count * hidden),
        name="middle_two",
    )(a2, unit, slope, x1, e, o, w2, w1, wo, vec, wide)


def input_body(dq_ref, dk_ref, dv_ref, x_ref, dx1_ref, w_ref, vec_ref, out_ref, sums_ref):
    @pl.when(pl.program_id(0) == 0)
    def _():
        sums_ref[...] = jnp.zeros_like(sums_ref)

    width = x_ref.shape[1]
    du = dot(dq_ref[...], w_ref[:, :width], (1, 1))
    du = du + dot(dk_ref[...], w_ref[:, width : 2 * width], (1, 1))
    du = du + dot(dv_ref[...], w_ref[:, 2 * width :], (1, 1))
    unit, scale = standardize(x_ref[...].astype(F32))
    sums_ref[0] += fold(du * unit)
    sums_ref[1] += fold(du)
    out_ref[...] = (dx1_ref[...] + norm_backward(du, vec_ref[0:1, :], unit, scale)).astype(BF)


def input_gradient(dq, dk, dv, x, dx1, w, vec):
    count, width = x.shape
    height = 512
    return pl.pallas_call(
        input_body,
        grid=(count // height,),
        in_specs=[rows(height, width)] * 5 + [whole(w.shape), whole(vec.shape)],
        out_specs=[rows(height, width), pl.BlockSpec((2, 8, width), lambda i: (0, 0, 0))],
        out_shape=[
            jax.ShapeDtypeStruct((count, width), BF),
            jax.ShapeDtypeStruct((2, 8, width), F32),
        ],
        compiler_params=params(),
        cost_estimate=cost(2 * count * w.size, 14 * count * width),
        name="input_gradient",
    )(dq, dk, dv, x, dx1, w, vec)


def renorm_body(x_ref, vec_ref, out_ref):
    unit, _ = standardize(x_ref[...].astype(F32))
    out_ref[...] = (unit * vec_ref[0:1, :] + vec_ref[1:2, :]).astype(BF)


def renorm(x, vec):
    count, width = x.shape
    height = 512
    return pl.pallas_call(
        renorm_body,
        grid=(count // height,),
        in_specs=[rows(height, width), whole(vec.shape)],
        out_specs=rows(height, width),
        out_shape=jax.ShapeDtypeStruct((count, width), BF),
        compiler_params=params(),
        name="renorm",
    )(x, vec)


def gather(shard, columns):
    return lax.all_gather(shard.reshape(-1, columns), "fsdp", axis=0, tiled=True)


def scatter(grad):
    return lax.psum_scatter(grad, "fsdp", scatter_dimension=0, tiled=True).astype(F32).reshape(-1)


def weight_gradient(a, b):
    return dot(a, b, (0, 0)).astype(BF)


def shards(hidden_in, doc_lens, w_qkv, w_out, w_fc1, w_fc2, vec_params, cotangent):
    micro_count, length, width = hidden_in.shape
    count = micro_count * length
    devices = lax.axis_size("fsdp")
    hidden = w_fc1.shape[0] * devices // width
    x = hidden_in.reshape(count, width)
    e = cotangent.reshape(count, width)
    lens = doc_lens.reshape(micro_count, doc_lens.shape[-1])

    vector = lax.all_gather(
        jnp.pad(vec_params, (0, -vec_params.shape[0] % 1024)).reshape(1, -1), "fsdp", axis=0, tiled=True
    )[:, : vec_params.shape[0]].reshape(-1).astype(F32)
    qkv_w = gather(w_qkv, 3 * width)
    out_w = gather(w_out, width)
    fc1_w = gather(w_fc1, hidden)
    fc2_w = gather(w_fc2, width)
    narrow = vector[: 9 * width].reshape(9, width)
    wide = vector[9 * width : 9 * width + 3 * hidden].reshape(3, hidden)
    last = vector[9 * width + 3 * hidden :].reshape(1, width)
    vec_one = narrow[0:4]
    vec_mid = jnp.concatenate([narrow[4:9], last], axis=0)

    qkv = project(x, qkv_w, vec_one)
    o, lse = attend(lens, qkv, length)
    a, x1, h2, a2, unit, slope = middle_one(o, x, out_w, fc1_w, vec_mid, wide)
    grad_fc2 = weight_gradient(a2, e)
    out, df, dx1, dr, do, inner, sums, wsums = middle_two(
        a2, unit, slope, x1, e, o, fc2_w, fc1_w, out_w, vec_mid, wide
    )
    grad_fc1 = weight_gradient(h2, df)
    grad_out = weight_gradient(a, dr)
    dq, dk, dv, bias_sums = attend_back(lens, qkv, do, lse, inner, length)
    normed = renorm(x, vec_one)
    grad_qkv = weight_gradient(normed, jnp.concatenate([dq, dk, dv], axis=1))
    grad_in, in_sums = input_gradient(dq, dk, dv, x, dx1, qkv_w, vec_one)

    sums = jnp.sum(sums, axis=1)
    wsums = jnp.sum(wsums, axis=1)
    in_sums = jnp.sum(in_sums, axis=1)
    bias_sums = jnp.sum(bias_sums, axis=0)
    grad_vec = jnp.concatenate(
        [
            in_sums[0], in_sums[1], bias_sums[0], bias_sums[2], sums[4], sums[5], sums[3], sums[1],
            sums[2], wsums[2], wsums[1], wsums[0], sums[0],
        ]
    )
    grad_vec = grad_vec.reshape(devices, -1)
    kept = grad_vec.shape[1]
    grad_vec = jnp.pad(grad_vec, ((0, 0), (0, -kept % 1024)))
    vec_share = lax.psum_scatter(grad_vec, "fsdp", scatter_dimension=0, tiled=True)[0, :kept]
    return (
        out.reshape(hidden_in.shape),
        grad_in.reshape(hidden_in.shape),
        scatter(grad_qkv),
        scatter(grad_out),
        scatter(grad_fc1),
        scatter(grad_fc2),
        vec_share,
    )


def solution(mesh):
    return jax.shard_map(
        shards,
        mesh=mesh,
        in_specs=(
            P(None, "fsdp", None),
            P(None, "fsdp", None),
            P("fsdp"),
            P("fsdp"),
            P("fsdp"),
            P("fsdp"),
            P("fsdp"),
            P(None, "fsdp", None),
        ),
        out_specs=(
            P(None, "fsdp", None),
            P(None, "fsdp", None),
            P("fsdp"),
            P("fsdp"),
            P("fsdp"),
            P("fsdp"),
            P("fsdp"),
        ),
        check_vma=False,
    )
```
